256 devices in a mesh: scen: 16 (over z, x_lo), pt: 16 (over x_hi, y, core).
Axes of the slice: x: 4 (x_hi: 2, x_lo: 2; x = x_hi * 2 + x_lo), y: 4, z: 8, core: 2. Of those that a mesh axis runs over, the one named last changes fastest.
Arguments:
- slip_counts: int32 [2048, 2048], P('scen'), may hold values from 0 to 7
- spectra: bfloat16 [2048, 4, 4096], P('scen', None, 'pt'), may hold values from -0.125 to 0.125
- transfer: bfloat16 [4096, 4, 2048], P('pt', None, 'scen'), may hold values from -0.09375 to 0.09375
- coast_owner: int32 [2048], P('pt'), may hold values from 0 to 127
Outputs:
- coast: bfloat16 [2048, 4, 2048], P('scen', None, 'pt')
- region_energy: float32 [2048, 128], P('scen')
The draws below stay inside these ranges and needn't reach their ends.
All inputs are finite; a program needn't handle non-finite values.
Results may differ from the reference program's by a relative error of at most 0.015.
Values may be sent and summed in bfloat16 or wider, within the bound.
A program may use at most 64 MiB of HBM per device.

```python
import jax
import jax.numpy as jnp
from jax import lax

U = 2048
P_SIZE = 4096
C = 2048
FREQ = 2
REGIONS = 128
S = 2048
N_PT = 16


def set_ends(values, key, least, top_value):
    index_at = [jax.random.randint(jax.random.fold_in(key, axis), (), 0, length) for axis, length in enumerate(values.shape)]
    widest = values.shape.index(max(values.shape))
    next_to = index_at[:widest] + [(index_at[widest] + 1) % values.shape[widest]] + index_at[widest + 1:]
    return values.at[tuple(index_at)].set(least).at[tuple(next_to)].set(top_value)


def spiked(array, key, source, target, parts, factor):
    owner, partner = [(jnp.arange(array.shape[position]) // (array.shape[position] // parts)).reshape([-1 if axis == position else 1 for axis in range(array.ndim)]) for position in (source, target)]
    chosen = jax.random.permutation(key, parts)[partner]
    strong = (owner == chosen) | (owner == (partner + parts // 2) % parts)
    return jnp.where(strong, factor * array, array)


def block_scale(stream_key, dims, split, least, top_value):
    def one(dim, parts):
        draws = jax.random.uniform(jax.random.fold_in(jax.random.fold_in(stream_key, 6), dim), (parts,), jnp.float32, least / len(split), top_value / len(split))
        return jnp.repeat(jnp.exp(draws), dims[dim] // parts).reshape((-1,) + (1,) * (len(dims) - dim - 1))

    loudness = one(*split[0])
    for cut in split[1:]:
        loudness = loudness * one(*cut)
    return loudness


def normal_values(key, extent, spread, bound, shards=(), held_as=jnp.bfloat16):
    drawn = spread * jax.random.normal(key, extent, jnp.float32)
    if shards:
        drawn = drawn * block_scale(key, extent, shards, -0.22, 0.18)
    return jnp.clip(drawn, -bound, bound).astype(held_as)


def gaussian_with(own_key, shape, width, limit, shards, heavy, held_as=jnp.bfloat16):
    array = width * jax.random.normal(own_key, shape, jnp.float32)
    if shards:
        array = array * block_scale(own_key, shape, shards, -0.22, 0.18)
    return jnp.clip(spiked(array, jax.random.fold_in(own_key, 3), *heavy), -limit, limit).astype(held_as)


def setup_inputs(seed: int = 0) -> dict:
    key_of = jax.random.split(jax.random.key(seed), 5)
    return {
        "slip_counts": set_ends(jax.random.randint(key_of[0], (S, U), 0, 8), jax.random.fold_in(key_of[0], 1), 0, 7).astype(jnp.int32),
        "spectra": normal_values(key_of[1], (U, 2 * FREQ, P_SIZE), U ** -0.5, 0.125, ((0, 16), (2, 16))),
        "transfer": gaussian_with(key_of[2], (P_SIZE, 2 * FREQ, C), (2 * P_SIZE) ** -0.5, 0.09375, ((0, 16), (2, 16)), (0, 2, 16, 2.0)),
        "coast_owner": set_ends(jax.random.randint(key_of[3], (C,), 0, REGIONS), jax.random.fold_in(key_of[3], 1), 0, REGIONS - 1).astype(jnp.int32),
    }


slip_step = 0.25


def coast_block(field_block, trans_block):
    outputs = []
    for freq in range(2):
        field_re = field_block[:, 2 * freq, :]
        field_im = field_block[:, 2 * freq + 1, :]
        real_left = jnp.stack([field_re, -field_im], axis=-1)
        imag_left = jnp.stack([field_im, field_re], axis=-1)
        left_both = jnp.stack([real_left, imag_left], axis=0)
        trans_pair = trans_block[:, 2 * freq:2 * freq + 2, :]
        product = jnp.einsum("xspc,pcd->sxd", left_both.astype(jnp.float32), trans_pair.astype(jnp.float32))
        outputs.append(product)
    return jnp.concatenate(outputs, axis=1)


def reference(slip_counts, spectra, transfer, coast_owner):
    weights = (slip_counts.astype(jnp.float32) * slip_step).astype(jnp.bfloat16)
    units, comps, points = spectra.shape
    field = jnp.dot(weights, spectra.reshape(units, comps * points), preferred_element_type=jnp.float32)
    field = field.astype(jnp.bfloat16).reshape(weights.shape[0], comps, points)
    block_len = points // N_PT
    total = jnp.zeros((weights.shape[0], comps, transfer.shape[2]), jnp.float32)
    for block in range(N_PT):
        lower = block * block_len
        part_sum = coast_block(field[:, :, lower:lower + block_len], transfer[lower:lower + block_len])
        total = total + lax.optimization_barrier(part_sum.astype(jnp.bfloat16)).astype(jnp.float32)
    coast = total.astype(jnp.bfloat16)
    squares = jnp.sum(total * total, axis=1)
    onehot = (coast_owner[:, None] == jnp.arange(REGIONS, dtype=jnp.int32)[None, :]).astype(jnp.float32)
    energy = jnp.dot(squares, onehot, precision=lax.Precision.HIGHEST, preferred_element_type=jnp.float32)
    return coast, energy * (REGIONS / C)
```

```python
import jax
import jax.numpy as jnp
from jax import lax
from jax.experimental import pallas as pl
from jax.experimental.pallas import tpu as pltpu
from jax.sharding import PartitionSpec as P

REGIONS = 128
SLIP_STEP = 0.25
NZ = 8
NY = 4
N_PT = 16
BF16 = jnp.bfloat16
F32 = jnp.float32
MESH = pl.DeviceIdType.MESH


def kernel(
    slip_ref, x_ref, t_ref, owner_ref, coast_ref, energy_ref,
    xr, tt, wb, gp, ry, rx, sx, hx, ga, acc, ob, co, en, eb, es, eo,
    s_first, s_ring, s_w, s_part, s_xh, s_gring, s_out, s_e, s_f, s_local,
    r_x, r_t, r_w, r_y, r_xh, r_g, r_c, r_e, r_f,
):
    i = lax.axis_index("scen")
    j = lax.axis_index("pt")
    z, xl = i // 2, lax.rem(i, 2)
    xh, y, f = j // 8, lax.rem(j // 2, 4), lax.rem(j, 2)
    g = 1 - f
    up, down = lax.rem(z + 1, NZ), lax.rem(z + NZ - 1, NZ)
    i_up, i_down, i_x = up * 2 + xl, down * 2 + xl, z * 2 + 1 - xl
    j_core = j - f + g
    j_xh = (1 - xh) * 8 + y * 2 + f

    barrier = pltpu.get_barrier_semaphore()

    def greet(a, b):
        pl.semaphore_signal(barrier, inc=1, device_id=(a, b), device_id_type=MESH)

    for a in (i_up, i_down, i_x):
        greet(a, j)
        greet(a, j_core)

    @pl.loop(1, N_PT)
    def _(d):
        greet(i, lax.rem(j + d, N_PT))

    pl.semaphore_wait(barrier, 6 + N_PT - 1)

    def remote(src, dst, s_sem, r_sem, a, b):
        return pltpu.make_async_remote_copy(
            src_ref=src, dst_ref=dst, send_sem=s_sem, recv_sem=r_sem,
            device_id=(a, b), device_id_type=MESH,
        )

    def arrived(dst, r_sem):
        remote(dst, dst, s_local.at[0], r_sem, i, j_core).wait_recv()

    first = [
        remote(t_ref.at[f], tt.at[7, f], s_first.at[0], r_t.at[7, f], i_up, j),
        remote(t_ref.at[f], tt.at[1, f], s_first.at[1], r_t.at[1, f], i_down, j),
        remote(t_ref.at[g], tt.at[7, f], s_first.at[2], r_t.at[7, f], i_up, j_core),
        remote(t_ref.at[g], tt.at[1, f], s_first.at[3], r_t.at[1, f], i_down, j_core),
        remote(x_ref.at[f], xr.at[xl, f], s_first.at[4], r_x.at[xl, f], i_x, j),
        remote(x_ref.at[g], xr.at[xl, f], s_first.at[5], r_x.at[xl, f], i_x, j_core),
        remote(x_ref.at[g], xr.at[xl, f], s_first.at[6], r_x.at[xl, f], i, j_core),
        remote(t_ref.at[g], tt.at[0, f], s_first.at[7], r_t.at[0, f], i, j_core),
    ]
    for copy in first:
        copy.start()
    local = [
        pltpu.make_async_copy(x_ref.at[f], xr.at[xl, f], s_local.at[1]),
        pltpu.make_async_copy(t_ref.at[f], tt.at[0, f], s_local.at[2]),
    ]
    for copy in local:
        copy.start()

    for block in range(NZ):
        counts = slip_ref[:, block * 256 : (block + 1) * 256]
        wb[xl, block] = (counts.astype(F32) * SLIP_STEP).astype(BF16)
    w_copy = remote(wb.at[xl], wb.at[xl], s_w.at[0], r_w.at[0], i_x, j)
    w_copy.start()

    for copy in local:
        copy.wait()
    arrived(xr.at[xl, g], r_x.at[xl, g])
    arrived(xr.at[1 - xl, 0], r_x.at[1 - xl, 0])
    arrived(xr.at[1 - xl, 1], r_x.at[1 - xl, 1])
    arrived(tt.at[0, g], r_t.at[0, g])

    def part_copy(slot):
        owner = lax.rem(z + slot, NZ)
        owner_y, owner_xh = lax.rem(owner, NY), owner // NY
        place = lax.rem(y - owner_y + NY, NY) - 1
        place = jnp.maximum(place, 0)
        return owner_y != y, remote(
            gp.at[slot], ry.at[owner_xh, place], s_part.at[slot], r_y.at[owner_xh, place],
            i, xh * 8 + owner_y * 2 + f,
        )

    def transfer_product(slot):
        for half in range(2):
            prod = jnp.dot(
                xr[half, 0].reshape(256, 256), tt[slot, 0], preferred_element_type=F32
            ) + jnp.dot(xr[half, 1].reshape(256, 256), tt[slot, 1], preferred_element_type=F32)
            rows = slice(half * 128, half * 128 + 128)
            gp[slot, rows, 0:128] = (prod[:128, :128] - prod[128:, 128:]).astype(BF16)
            gp[slot, rows, 128:256] = (prod[:128, 128:] + prod[128:, :128]).astype(BF16)
        away, copy = part_copy(slot)

        @pl.when(away)
        def _():
            copy.start()

    def ring(buf, r_sem, s_sem, use):
        sent = []

        def forward(src_slot, dst_slot, piece, a, n):
            copy = remote(
                buf.at[src_slot, piece], buf.at[dst_slot, piece],
                s_sem.at[n], r_sem.at[dst_slot, piece], a, j,
            )
            copy.start()
            sent.append(copy)

        n = 0
        for step in range(1, 4):
            for piece in range(2):
                for slot, ahead, a in ((8 - step, 7 - step, i_up), (step, step + 1, i_down)):
                    arrived(buf.at[slot, piece], r_sem.at[slot, piece])
                    if step < 3 or piece == (0 if slot > 4 else 1):
                        forward(slot, ahead, piece, a, n)
                        n += 1
            use(8 - step)
            use(step)
        for piece in range(2):
            arrived(buf.at[4, piece], r_sem.at[4, piece])
        use(4)
        return sent

    transfer_product(0)
    sent = ring(tt, r_t, s_ring, transfer_product)

    def summed(h):
        for k in range(NY - 1):
            arrived(ry.at[h, k], r_y.at[h, k])
        own = lax.rem(h * NY + y - z + NZ, NZ)
        total = gp[own].astype(F32)
        for k in range(NY - 1):
            total = total + ry[h, k].astype(F32)
        return total

    sx[...] = summed(1 - xh).astype(BF16)
    xh_copy = remote(sx, rx, s_xh.at[0], r_xh.at[0], i, j_xh)
    xh_copy.start()
    hx[...] = summed(xh)
    arrived(rx, r_xh.at[0])
    for half in range(2):
        rows = slice(half * 128, half * 128 + 128)
        ga[0, half] = (hx[rows, :] + rx[rows, :].astype(F32)).astype(BF16)
    g_first = []
    for half in range(2):
        g_first.append(
            remote(ga.at[0, half], ga.at[7, half], s_gring.at[10 + half], r_g.at[7, half], i_up, j)
        )
        g_first.append(
            remote(ga.at[0, half], ga.at[1, half], s_gring.at[12 + half], r_g.at[1, half], i_down, j)
        )
    for copy in g_first:
        copy.start()

    arrived(wb.at[1 - xl], r_w.at[0])

    def weigh(slot, fresh=False):
        block = lax.rem(z + slot, NZ)
        for half in range(2):
            prod = jnp.dot(
                wb[half, block], ga[slot].reshape(256, 256), preferred_element_type=F32
            )
            if fresh:
                acc[half] = prod
            else:
                acc[half] += prod

    weigh(0, fresh=True)
    sent += ring(ga, r_g, s_gring, weigh)

    for half in range(2):
        ob[half] = acc[half].astype(BF16)
    j_out = xh * 8 + y * 2 + xl
    out_far = remote(ob.at[1 - xl], co.at[f], s_out.at[0], r_c.at[f], i_x, j_out)
    out_far.start()
    out_near = remote(ob.at[xl], co.at[f], s_out.at[1], r_c.at[f], i, j_core)

    @pl.when(f != xl)
    def _():
        out_near.start()
        arrived(co.at[f], r_c.at[f])

    @pl.when(f == xl)
    def _():
        co[f] = ob[xl]

    arrived(co.at[g], r_c.at[g])

    squares = jnp.zeros((128, 128), F32)
    for freq in range(2):
        part = co[freq]
        coast_ref[:, freq * 256 : freq * 256 + 256] = part
        wide = part.astype(F32)
        squares = squares + wide[:, :128] * wide[:, :128] + wide[:, 128:] * wide[:, 128:]
    region = lax.broadcasted_iota(jnp.int32, (REGIONS, 128), 0)
    onehot = (owner_ref[...] == region).astype(F32)
    en[...] = lax.dot_general(
        squares, onehot, (((1,), (1,)), ((), ())),
        precision=lax.Precision.HIGHEST, preferred_element_type=F32,
    ).reshape(N_PT, 8, 128)

    def e_copy(d):
        b = lax.rem(j + d, N_PT)
        return remote(en.at[b], eb.at[j], s_e.at[d], r_e.at[j], i, b)

    def f_copy(d):
        return remote(es, eo.at[j], s_f.at[d], r_f.at[j], i, lax.rem(j + d, N_PT))

    @pl.loop(1, N_PT)
    def _(d):
        e_copy(d).start()

    eb[j] = en[j]

    @pl.loop(1, N_PT)
    def _(d):
        b = lax.rem(j + d, N_PT)
        arrived(eb.at[b], r_e.at[b])

    es[...] = jnp.sum(eb[...], axis=0) * (REGIONS / 2048)

    @pl.loop(1, N_PT)
    def _(d):
        f_copy(d).start()

    eo[j] = es[...]

    @pl.loop(1, N_PT)
    def _(d):
        b = lax.rem(j + d, N_PT)
        arrived(eo.at[b], r_f.at[b])

    energy_ref[...] = eo[...].reshape(128, REGIONS)

    for copy in first + [w_copy] + sent + [xh_copy] + g_first + [out_far]:
        copy.wait_send()
    for slot in range(NZ):
        away, copy = part_copy(slot)

        @pl.when(away)
        def _():
            copy.wait_send()

    @pl.when(f != xl)
    def _():
        out_near.wait_send()

    @pl.loop(1, N_PT)
    def _(d):
        e_copy(d).wait_send()
        f_copy(d).wait_send()


def per_device(slip_counts, spectra, transfer, coast_owner):
    x = spectra.reshape(128, 2, 2, 256).transpose(1, 2, 0, 3)
    t = transfer.reshape(256, 2, 256).transpose(1, 0, 2)
    owner = coast_owner.reshape(1, 128)
    vmem = pl.BlockSpec(memory_space=pltpu.VMEM)
    dma = pltpu.SemaphoreType.DMA
    coast, energy = pl.pallas_call(
        kernel,
        out_shape=(
            jax.ShapeDtypeStruct((128, 512), BF16),
            jax.ShapeDtypeStruct((128, REGIONS), F32),
        ),
        in_specs=[vmem] * 4,
        out_specs=[vmem] * 2,
        scratch_shapes=[
            pltpu.VMEM((2, 2, 2, 128, 256), BF16),
            pltpu.VMEM((NZ, 2, 256, 256), BF16),
            pltpu.VMEM((2, NZ, 128, 256), BF16),
            pltpu.VMEM((NZ, 256, 256), BF16),
            pltpu.VMEM((2, NY - 1, 256, 256), BF16),
            pltpu.VMEM((256, 256), BF16),
            pltpu.VMEM((256, 256), BF16),
            pltpu.VMEM((256, 256), F32),
            pltpu.VMEM((NZ, 2, 128, 256), BF16),
            pltpu.VMEM((2, 128, 256), F32),
            pltpu.VMEM((2, 128, 256), BF16),
            pltpu.VMEM((2, 128, 256), BF16),
            pltpu.VMEM((N_PT, 8, 128), F32),
            pltpu.VMEM((N_PT, 8, 128), F32),
            pltpu.VMEM((8, 128), F32),
            pltpu.VMEM((N_PT, 8, 128), F32),
            dma((8,)),
            dma((10,)),
            dma((1,)),
            dma((NZ,)),
            dma((1,)),
            dma((14,)),
            dma((2,)),
            dma((N_PT,)),
            dma((N_PT,)),
            dma((3,)),
            dma((2, 2)),
            dma((NZ, 2)),
            dma((1,)),
            dma((2, NY - 1)),
            dma((1,)),
            dma((NZ, 2)),
            dma((2,)),
            dma((N_PT,)),
            dma((N_PT,)),
        ],
        compiler_params=pltpu.CompilerParams(collective_id=0, has_side_effects=True),
    )(slip_counts, x, t, owner)
    return coast.reshape(128, 4, 128), energy


def solution(mesh):
    placed = (P("scen", None), P("scen", None, "pt"), P("pt", None, "scen"), P("pt"))
    return jax.shard_map(
        per_device,
        mesh=mesh,
        in_specs=placed,
        out_specs=(P("scen", None, "pt"), P("scen", None)),
        check_vma=False,
    )
```

```python
import jax
import jax.numpy as jnp
from jax import lax
from jax.experimental import pallas as pl
from jax.experimental.pallas import tpu as pltpu
from jax.sharding import PartitionSpec as P

REGIONS = 128
SLIP_STEP = 0.25
NZ = 8
NY = 4
N_PT = 16
BF16 = jnp.bfloat16
F32 = jnp.float32
MESH = pl.DeviceIdType.MESH


def kernel(
    slip_hbm, x_hbm, t_hbm, owner_ref, coast_ref, energy_ref,
    slip, x_raw, t_raw, xs, ts, xr, tt, wb, gp, ry, rx, sx, hx, ga, acc, ob, co, own,
    en, eb, es, eo,
    s_first, s_ring, s_w, s_part, s_xh, s_gring, s_out, s_e, s_f, s_local,
    r_x, r_t, r_w, r_y, r_xh, r_g, r_c, r_e, r_f, r_own,
):
    i = lax.axis_index("scen")
    j = lax.axis_index("pt")
    z, xl = i // 2, lax.rem(i, 2)
    xh, y, f = j // 8, lax.rem(j // 2, 4), lax.rem(j, 2)
    g = 1 - f
    up, down = lax.rem(z + 1, NZ), lax.rem(z + NZ - 1, NZ)
    i_up, i_down, i_x = up * 2 + xl, down * 2 + xl, z * 2 + 1 - xl
    j_core = j - f + g
    j_xh = (1 - xh) * 8 + y * 2 + f

    barrier = pltpu.get_barrier_semaphore()

    def greet(a, b):
        pl.semaphore_signal(barrier, inc=1, device_id=(a, b), device_id_type=MESH)

    loads = [
        pltpu.make_async_copy(t_hbm, t_raw, s_local.at[3]),
        pltpu.make_async_copy(x_hbm, x_raw, s_local.at[4]),
        pltpu.make_async_copy(slip_hbm, slip, s_local.at[5]),
    ]
    for copy in loads:
        copy.start()
    for a in (i_up, i_down):
        greet(a, j)
        greet(a, j_core)
    greet(i_x, j)

    @pl.loop(1, N_PT)
    def _(d):
        greet(i, lax.rem(j + d, N_PT))
        greet(i_x, lax.rem(j + d, N_PT))

    def remote(src, dst, s_sem, r_sem, a, b):
        return pltpu.make_async_remote_copy(
            src_ref=src, dst_ref=dst, send_sem=s_sem, recv_sem=r_sem,
            device_id=(a, b), device_id_type=MESH,
        )

    def arrived(dst, r_sem):
        remote(dst, dst, s_local.at[0], r_sem, i, j_core).wait_recv()

    loads[0].wait()
    for k in range(4):
        part = t_raw[:, k, :]
        for half in range(2):
            ts[k // 2, half, :, (k % 2) * 128 : (k % 2) * 128 + 128] = part[
                half * 128 : half * 128 + 128
            ]
    loads[1].wait()
    for k in range(4):
        xs[k // 2, k % 2] = x_raw[:, k, :]
    own[f] = owner_ref[...]

    pl.semaphore_wait(barrier, 5 + 2 * (N_PT - 1))

    first = []
    for half in range(2):
        for slot, a in ((7, i_up), (1, i_down)):
            first.append((ts.at[f, half], tt.at[slot, f, half], r_t.at[slot, f, half], a, j))
    for half in range(2):
        for slot, a in ((7, i_up), (1, i_down)):
            first.append((ts.at[g, half], tt.at[slot, f, half], r_t.at[slot, f, half], a, j_core))
    first.append((xs.at[f], xr.at[xl, f], r_x.at[xl, f], i_x, j))
    first.append((xs.at[g], xr.at[xl, f], r_x.at[xl, f], i_x, j_core))
    first.append((xs.at[g], xr.at[xl, f], r_x.at[xl, f], i, j_core))
    for half in range(2):
        first.append((ts.at[g, half], tt.at[0, f, half], r_t.at[0, f, half], i, j_core))
    first.append((own.at[f], own.at[f], r_own.at[0], i, j_core))
    first = [
        remote(src, dst, s_first.at[n], r_sem, a, b)
        for n, (src, dst, r_sem, a, b) in enumerate(first)
    ]
    for copy in first:
        copy.start()
    local = [
        pltpu.make_async_copy(xs.at[f], xr.at[xl, f], s_local.at[1]),
        pltpu.make_async_copy(ts.at[f], tt.at[0, f], s_local.at[2]),
    ]
    for copy in local:
        copy.start()

    loads[2].wait()
    for block in range(NZ):
        counts = slip[:, block * 256 : (block + 1) * 256]
        wb[block, xl] = (counts.astype(F32) * SLIP_STEP).astype(BF16)
    w_copy = remote(wb.at[:, xl], wb.at[:, xl], s_w.at[0], r_w.at[0], i_x, j)
    w_copy.start()

    def part_copy(slot, half):
        owner = lax.rem(z + slot, NZ)
        owner_y, owner_xh = lax.rem(owner, NY), owner // NY
        place = jnp.maximum(lax.rem(y - owner_y + NY, NY) - 1, 0)
        return owner_y != y, remote(
            gp.at[slot, half], ry.at[owner_xh, place, half], s_part.at[slot, half],
            r_y.at[owner_xh, place, half], i, xh * 8 + owner_y * 2 + f,
        )

    def transfer_product(slot):
        for half in range(2):
            prod = jnp.dot(
                xr[half, 0].reshape(256, 256), tt[slot, 0].reshape(256, 256),
                preferred_element_type=F32,
            ) + jnp.dot(
                xr[half, 1].reshape(256, 256), tt[slot, 1].reshape(256, 256),
                preferred_element_type=F32,
            )
            gp[slot, half, :, 0:128] = (prod[:128, :128] - prod[128:, 128:]).astype(BF16)
            gp[slot, half, :, 128:256] = (prod[:128, 128:] + prod[128:, :128]).astype(BF16)
            away, copy = part_copy(slot, half)

            @pl.when(away)
            def _():
                copy.start()

    sent = []

    def forward(buf, r_sem, s_sem, n, src_slot, dst_slot, piece, a):
        copy = remote(
            buf.at[(src_slot,) + piece], buf.at[(dst_slot,) + piece],
            s_sem.at[n], r_sem.at[(dst_slot,) + piece], a, j,
        )
        copy.start()
        sent.append(copy)

    def ring(buf, r_sem, s_sem, pieces, work):
        n = 0
        for step in range(1, 4):
            for k, piece in enumerate(pieces):
                for slot, ahead, a in ((8 - step, 7 - step, i_up), (step, step + 1, i_down)):
                    at = (slot,) + piece
                    arrived(buf.at[at], r_sem.at[at])
                    first_half = k < len(pieces) // 2
                    if step < 3 or first_half == (slot > 4):
                        forward(buf, r_sem, s_sem, n, slot, ahead, piece, a)
                        n += 1
                work(step, k)
        half = len(pieces) // 2
        for k in range(half):
            for piece in (pieces[k], pieces[k + half]):
                at = (4,) + piece
                arrived(buf.at[at], r_sem.at[at])
            work(4, k)

    def transfer_work(step, k):
        if step == 1 and k == 3:
            for copy in local:
                copy.wait()
            arrived(xr.at[xl, g], r_x.at[xl, g])
            for c in range(2):
                arrived(xr.at[1 - xl, c], r_x.at[1 - xl, c])
                arrived(tt.at[0, g, c], r_t.at[0, g, c])
        plan = {
            (2, 0): 0, (2, 1): 7, (2, 3): 1, (3, 1): 6, (3, 3): 2, (4, 0): 5, (4, 1): 3,
        }
        if (step, k) in plan:
            transfer_product(plan[(step, k)])

    ring(tt, r_t, s_ring, [(f, 0), (f, 1), (g, 0), (g, 1)], transfer_work)
    transfer_product(4)

    def summed(h, half):
        for k in range(NY - 1):
            arrived(ry.at[h, k, half], r_y.at[h, k, half])
        mine = lax.rem(h * NY + y - z + NZ, NZ)
        total = gp[mine, half].astype(F32)
        for k in range(NY - 1):
            total = total + ry[h, k, half].astype(F32)
        return total

    xh_copies = []
    for half in range(2):
        sx[half] = summed(1 - xh, half).astype(BF16)
        copy = remote(sx.at[half], rx.at[half], s_xh.at[half], r_xh.at[half], i, j_xh)
        copy.start()
        xh_copies.append(copy)
    for half in range(2):
        hx[half] = summed(xh, half)
    g_first = []
    for half in range(2):
        arrived(rx.at[half], r_xh.at[half])
        for q in range(2):
            p = half * 2 + q
            rows = slice(q * 64, q * 64 + 64)
            ga[0, p] = (hx[half, rows, :] + rx[half, rows, :].astype(F32)).astype(BF16)
            for n, (slot, a) in enumerate(((7, i_up), (1, i_down))):
                copy = remote(
                    ga.at[0, p], ga.at[slot, p], s_gring.at[20 + 2 * p + n], r_g.at[slot, p], a, j
                )
                copy.start()
                g_first.append(copy)

    arrived(wb.at[:, 1 - xl], r_w.at[0])

    def weigh(slot):
        block = lax.rem(z + slot, NZ)
        prod = jnp.dot(
            wb[block].reshape(256, 256), ga[slot].reshape(256, 256), preferred_element_type=F32
        )
        if slot == 0:
            acc[...] = prod
        else:
            acc[...] += prod

    def weigh_work(step, k):
        plan = {(1, 0): 0, (2, 0): 7, (2, 2): 1, (3, 0): 6, (3, 2): 2, (4, 0): 5}
        if (step, k) in plan:
            weigh(plan[(step, k)])

    ring(ga, r_g, s_gring, [(0,), (1,), (2,), (3,)], weigh_work)
    weigh(3)
    weigh(4)

    total = acc[...]
    for half in range(2):
        ob[half] = total[half * 128 : half * 128 + 128].astype(BF16)
    j_out = xh * 8 + y * 2 + xl
    out_far = remote(ob.at[1 - xl], co.at[f], s_out.at[0], r_c.at[f], i_x, j_out)
    out_far.start()
    out_near = remote(ob.at[xl], co.at[f], s_out.at[1], r_c.at[f], i, j_core)

    @pl.when(f != xl)
    def _():
        out_near.start()

    squares = total[:, :128] * total[:, :128] + total[:, 128:] * total[:, 128:]
    region = lax.broadcasted_iota(jnp.int32, (REGIONS, 128), 0)
    arrived(own.at[g], r_own.at[0])
    onehot = (own[xl] == region).astype(F32).astype(BF16)
    top = squares.astype(BF16)
    rest = (squares - top.astype(F32)).astype(BF16)
    dims = (((1,), (1,)), ((), ()))
    energy = lax.dot_general(top, onehot, dims, preferred_element_type=F32) + lax.dot_general(
        rest, onehot, dims, preferred_element_type=F32
    )
    en[...] = energy.reshape(2, N_PT, 8, 128)

    def e_copy(side, d):
        b = lax.rem(j + d, N_PT)
        return remote(
            en.at[jnp.abs(xl - side), b], eb.at[side, j], s_e.at[side, d], r_e.at[side, j],
            z * 2 + jnp.abs(xl - side), b,
        )

    def f_copy(d):
        return remote(es, eo.at[j], s_f.at[d], r_f.at[j], i, lax.rem(j + d, N_PT))

    @pl.loop(1, N_PT)
    def _(d):
        e_copy(0, d).start()
        e_copy(1, d).start()

    e_copy(1, 0).start()
    eb[0, j] = en[xl, j]

    @pl.when(f != xl)
    def _():
        arrived(co.at[f], r_c.at[f])

    @pl.when(f == xl)
    def _():
        co[f] = ob[xl]

    arrived(co.at[g], r_c.at[g])
    for freq in range(2):
        for comp in range(2):
            coast_ref[:, freq * 2 + comp, :] = co[freq, :, comp * 128 : comp * 128 + 128]

    arrived(eb.at[1, j], r_e.at[1, j])

    @pl.loop(1, N_PT)
    def _(d):
        b = lax.rem(j + d, N_PT)
        arrived(eb.at[0, b], r_e.at[0, b])
        arrived(eb.at[1, b], r_e.at[1, b])

    es[...] = jnp.sum(eb[...].reshape(2 * N_PT, 8, 128), axis=0) * (REGIONS / 2048)

    @pl.loop(1, N_PT)
    def _(d):
        f_copy(d).start()

    eo[j] = es[...]
    for copy in first + [w_copy] + sent + xh_copies + g_first + [out_far]:
        copy.wait_send()
    for slot in range(NZ):
        for half in range(2):
            away, copy = part_copy(slot, half)

            @pl.when(away)
            def _():
                copy.wait_send()

    @pl.when(f != xl)
    def _():
        out_near.wait_send()

    e_copy(1, 0).wait_send()

    @pl.loop(1, N_PT)
    def _(d):
        b = lax.rem(j + d, N_PT)
        arrived(eo.at[b], r_f.at[b])

    energy_ref[...] = eo[...].reshape(128, REGIONS)

    @pl.loop(1, N_PT)
    def _(d):
        e_copy(0, d).wait_send()
        e_copy(1, d).wait_send()
        f_copy(d).wait_send()


def per_device(slip_counts, spectra, transfer, coast_owner):
    owner = coast_owner.reshape(1, 128)
    vmem = pl.BlockSpec(memory_space=pltpu.VMEM)
    hbm = pl.BlockSpec(memory_space=pl.ANY)
    dma = pltpu.SemaphoreType.DMA
    coast, energy = pl.pallas_call(
        kernel,
        out_shape=(
            jax.ShapeDtypeStruct((128, 4, 128), BF16),
            jax.ShapeDtypeStruct((128, REGIONS), F32),
        ),
        in_specs=[hbm] * 3 + [vmem],
        out_specs=[vmem] * 2,
        scratch_shapes=[
            pltpu.VMEM((128, 2048), jnp.int32),
            pltpu.VMEM((128, 4, 256), BF16),
            pltpu.VMEM((256, 4, 128), BF16),
            pltpu.VMEM((2, 2, 128, 256), BF16),
            pltpu.VMEM((2, 2, 128, 256), BF16),
            pltpu.VMEM((2, 2, 2, 128, 256), BF16),
            pltpu.VMEM((NZ, 2, 2, 128, 256), BF16),
            pltpu.VMEM((NZ, 2, 128, 256), BF16),
            pltpu.VMEM((NZ, 2, 128, 256), BF16),
            pltpu.VMEM((2, NY - 1, 2, 128, 256), BF16),
            pltpu.VMEM((2, 128, 256), BF16),
            pltpu.VMEM((2, 128, 256), BF16),
            pltpu.VMEM((2, 128, 256), F32),
            pltpu.VMEM((NZ, 4, 64, 256), BF16),
            pltpu.VMEM((256, 256), F32),
            pltpu.VMEM((2, 128, 256), BF16),
            pltpu.VMEM((2, 128, 256), BF16),
            pltpu.VMEM((2, 1, 128), jnp.int32),
            pltpu.VMEM((2, N_PT, 8, 128), F32),
            pltpu.VMEM((2, N_PT, 8, 128), F32),
            pltpu.VMEM((8, 128), F32),
            pltpu.VMEM((N_PT, 8, 128), F32),
            dma((14,)),
            dma((20,)),
            dma((1,)),
            dma((NZ, 2)),
            dma((2,)),
            dma((28,)),
            dma((2,)),
            dma((2, N_PT)),
            dma((N_PT,)),
            dma((6,)),
            dma((2, 2)),
            dma((NZ, 2, 2)),
            dma((1,)),
            dma((2, NY - 1, 2)),
            dma((2,)),
            dma((NZ, 4)),
            dma((2,)),
            dma((2, N_PT)),
            dma((N_PT,)),
            dma((1,)),
        ],
        compiler_params=pltpu.CompilerParams(collective_id=0, has_side_effects=True),
    )(slip_counts, spectra, transfer, owner)
    return coast, energy


def solution(mesh):
    placed = (P("scen", None), P("scen", None, "pt"), P("pt", None, "scen"), P("pt"))
    return jax.shard_map(
        per_device,
        mesh=mesh,
        in_specs=placed,
        out_specs=(P("scen", None, "pt"), P("scen", None)),
        check_vma=False,
    )
```

```python
import jax
import jax.numpy as jnp
from jax import lax
from jax.experimental import pallas as pl
from jax.experimental.pallas import tpu as pltpu
from jax.sharding import PartitionSpec as P

REGIONS = 128
SLIP_STEP = 0.25
NZ = 8
NY = 4
N_PT = 16
BF16 = jnp.bfloat16
F32 = jnp.float32
MESH = pl.DeviceIdType.MESH


def kernel(
    slip_hbm, x_hbm, t_hbm, owner_ref, coast_ref, energy_ref,
    slip, x_raw, t_raw, xs, ts, xr, tt, wb, gp, ry, rx, sx, hx, ga, acc, ob, co, own,
    en, eb, es, eo,
    s_all, s_local,
    r_x, r_t, r_w, r_y, r_xh, r_g, r_c, r_e, r_f, r_own,
):
    i = lax.axis_index("scen")
    j = lax.axis_index("pt")
    z, xl = i // 2, lax.rem(i, 2)
    xh, y, f = j // 8, lax.rem(j // 2, 4), lax.rem(j, 2)
    g = 1 - f
    up, down = lax.rem(z + 1, NZ), lax.rem(z + NZ - 1, NZ)
    i_up, i_down, i_x = up * 2 + xl, down * 2 + xl, z * 2 + 1 - xl
    j_core = j - f + g
    j_xh = (1 - xh) * 8 + y * 2 + f

    barrier = pltpu.get_barrier_semaphore()

    def greet(a, b):
        pl.semaphore_signal(barrier, inc=1, device_id=(a, b), device_id_type=MESH)

    loads = [
        pltpu.make_async_copy(t_hbm, t_raw, s_local.at[3]),
        pltpu.make_async_copy(x_hbm, x_raw, s_local.at[4]),
        pltpu.make_async_copy(slip_hbm, slip, s_local.at[5]),
    ]
    for copy in loads:
        copy.start()
    for a in (i_up, i_down):
        greet(a, j)
        greet(a, j_core)
    greet(i_x, j)

    @pl.loop(1, N_PT)
    def _(d):
        greet(i, lax.rem(j + d, N_PT))
        greet(i_x, lax.rem(j + d, N_PT))

    def remote(src, dst, r_sem, a, b):
        return pltpu.make_async_remote_copy(
            src_ref=src, dst_ref=dst, send_sem=s_all.at[0], recv_sem=r_sem,
            device_id=(a, b), device_id_type=MESH,
        )

    def arrived(dst, r_sem):
        remote(dst, dst, r_sem, i, j_core).wait_recv()

    loads[0].wait()
    for k in range(4):
        part = t_raw[:, k, :]
        for half in range(2):
            ts[k // 2, half, :, (k % 2) * 128 : (k % 2) * 128 + 128] = part[
                half * 128 : half * 128 + 128
            ]
    loads[1].wait()
    for k in range(4):
        xs[k // 2, k % 2] = x_raw[:, k, :]
    own[f] = owner_ref[...]

    pl.semaphore_wait(barrier, 5 + 2 * (N_PT - 1))

    first = []
    for half in range(2):
        for slot, a in ((7, i_up), (1, i_down)):
            first.append((ts.at[f, half], tt.at[slot, f, half], r_t.at[slot, f, half], a, j))
    for half in range(2):
        for slot, a in ((7, i_up), (1, i_down)):
            first.append((ts.at[g, half], tt.at[slot, f, half], r_t.at[slot, f, half], a, j_core))
    first.append((xs.at[f], xr.at[xl, f], r_x.at[xl, f], i_x, j))
    first.append((xs.at[g], xr.at[xl, f], r_x.at[xl, f], i_x, j_core))
    first.append((xs.at[g], xr.at[xl, f], r_x.at[xl, f], i, j_core))
    for half in range(2):
        first.append((ts.at[g, half], tt.at[0, f, half], r_t.at[0, f, half], i, j_core))
    first.append((own.at[f], own.at[f], r_own.at[0], i, j_core))
    first = [
        remote(src, dst, r_sem, a, b) for src, dst, r_sem, a, b in first
    ]
    for copy in first:
        copy.start()
    local = [
        pltpu.make_async_copy(xs.at[f], xr.at[xl, f], s_local.at[1]),
        pltpu.make_async_copy(ts.at[f], tt.at[0, f], s_local.at[2]),
    ]
    for copy in local:
        copy.start()

    loads[2].wait()
    for block in range(NZ):
        counts = slip[:, block * 256 : (block + 1) * 256]
        wb[block, xl] = (counts.astype(F32) * SLIP_STEP).astype(BF16)
    w_copy = remote(wb.at[:, xl], wb.at[:, xl], r_w.at[0], i_x, j)
    w_copy.start()

    def part_copy(slot, half):
        owner = lax.rem(z + slot, NZ)
        owner_y, owner_xh = lax.rem(owner, NY), owner // NY
        place = jnp.maximum(lax.rem(y - owner_y + NY, NY) - 1, 0)
        return owner_y != y, remote(
            gp.at[slot, half], ry.at[owner_xh, place, half], r_y.at[owner_xh, place, half],
            i, xh * 8 + owner_y * 2 + f,
        )

    def transfer_product(slot):
        for half in range(2):
            prod = jnp.dot(
                xr[half, 0].reshape(256, 256), tt[slot, 0].reshape(256, 256),
                preferred_element_type=F32,
            ) + jnp.dot(
                xr[half, 1].reshape(256, 256), tt[slot, 1].reshape(256, 256),
                preferred_element_type=F32,
            )
            gp[slot, half, :, 0:128] = (prod[:128, :128] - prod[128:, 128:]).astype(BF16)
            gp[slot, half, :, 128:256] = (prod[:128, 128:] + prod[128:, :128]).astype(BF16)
            away, copy = part_copy(slot, half)

            @pl.when(away)
            def _():
                copy.start()

    sent = []

    def forward(buf, r_sem, src_slot, dst_slot, piece, a):
        copy = remote(
            buf.at[(src_slot,) + piece], buf.at[(dst_slot,) + piece],
            r_sem.at[(dst_slot,) + piece], a, j,
        )
        copy.start()
        sent.append(copy)

    def ring(buf, r_sem, pieces, work):
        for step in range(1, 4):
            for k, piece in enumerate(pieces):
                for slot, ahead, a in ((8 - step, 7 - step, i_up), (step, step + 1, i_down)):
                    at = (slot,) + piece
                    arrived(buf.at[at], r_sem.at[at])
                    first_half = k < len(pieces) // 2
                    if step < 3 or first_half == (slot > 4):
                        forward(buf, r_sem, slot, ahead, piece, a)
                work(step, k)
        half = len(pieces) // 2
        for k in range(half):
            for piece in (pieces[k], pieces[k + half]):
                at = (4,) + piece
                arrived(buf.at[at], r_sem.at[at])
            work(4, k)

    def transfer_work(step, k):
        if step == 1 and k == 3:
            for copy in local:
                copy.wait()
            arrived(xr.at[xl, g], r_x.at[xl, g])
            for c in range(2):
                arrived(xr.at[1 - xl, c], r_x.at[1 - xl, c])
                arrived(tt.at[0, g, c], r_t.at[0, g, c])
        plan = {
            (2, 0): 0, (2, 1): 7, (2, 3): 1, (3, 1): 6, (3, 3): 2, (4, 0): 5, (4, 1): 3,
        }
        if (step, k) in plan:
            transfer_product(plan[(step, k)])

    ring(tt, r_t, [(f, 0), (f, 1), (g, 0), (g, 1)], transfer_work)
    transfer_product(4)

    def summed(h, half):
        for k in range(NY - 1):
            arrived(ry.at[h, k, half], r_y.at[h, k, half])
        mine = lax.rem(h * NY + y - z + NZ, NZ)
        total = gp[mine, half].astype(F32)
        for k in range(NY - 1):
            total = total + ry[h, k, half].astype(F32)
        return total

    xh_copies = []
    for half in range(2):
        sx[half] = summed(1 - xh, half).astype(BF16)
        copy = remote(sx.at[half], rx.at[half], r_xh.at[half], i, j_xh)
        copy.start()
        xh_copies.append(copy)
    for half in range(2):
        hx[half] = summed(xh, half)
    g_first = []
    for half in range(2):
        arrived(rx.at[half], r_xh.at[half])
        for q in range(2):
            p = half * 2 + q
            rows = slice(q * 64, q * 64 + 64)
            ga[0, p] = (hx[half, rows, :] + rx[half, rows, :].astype(F32)).astype(BF16)
            for slot, a in ((7, i_up), (1, i_down)):
                copy = remote(ga.at[0, p], ga.at[slot, p], r_g.at[slot, p], a, j)
                copy.start()
                g_first.append(copy)

    arrived(wb.at[:, 1 - xl], r_w.at[0])

    def weigh(slot):
        block = lax.rem(z + slot, NZ)
        prod = jnp.dot(
            wb[block].reshape(256, 256), ga[slot].reshape(256, 256), preferred_element_type=F32
        )
        if slot == 0:
            acc[...] = prod
        else:
            acc[...] += prod

    def weigh_work(step, k):
        plan = {(1, 0): 0, (2, 0): 7, (2, 2): 1, (3, 0): 6, (3, 2): 2, (4, 0): 5}
        if (step, k) in plan:
            weigh(plan[(step, k)])

    ring(ga, r_g, [(0,), (1,), (2,), (3,)], weigh_work)
    weigh(3)
    weigh(4)

    total = acc[...]
    for half in range(2):
        ob[half] = total[half * 128 : half * 128 + 128].astype(BF16)
    j_out = xh * 8 + y * 2 + xl
    out_far = remote(ob.at[1 - xl], co.at[f], r_c.at[f], i_x, j_out)
    out_far.start()
    out_near = remote(ob.at[xl], co.at[f], r_c.at[f], i, j_core)

    @pl.when(f != xl)
    def _():
        out_near.start()

    squares = total[:, :128] * total[:, :128] + total[:, 128:] * total[:, 128:]
    region = lax.broadcasted_iota(jnp.int32, (REGIONS, 128), 0)
    arrived(own.at[g], r_own.at[0])
    onehot = (own[xl] == region).astype(F32).astype(BF16)
    top = squares.astype(BF16)
    rest = (squares - top.astype(F32)).astype(BF16)
    dims = (((1,), (1,)), ((), ()))
    energy = lax.dot_general(top, onehot, dims, preferred_element_type=F32) + lax.dot_general(
        rest, onehot, dims, preferred_element_type=F32
    )
    en[...] = energy.reshape(2, NZ, 16, 128)

    place = xh * NY + y

    def e_copy(side, d):
        h = jnp.abs(xl - side)
        b = lax.rem(place + d, NZ)
        return remote(
            en.at[h, b], eb.at[xl, j], r_e.at[0], z * 2 + h, b * 2 + h
        )

    e_copy(1, 0).start()

    @pl.loop(1, NZ)
    def _(d):
        e_copy(0, d).start()
        e_copy(1, d).start()

    e_own = pltpu.make_async_copy(en.at[xl, place], eb.at[xl, j], r_e.at[0])

    @pl.when(f != xl)
    def _():
        e_copy(0, 0).start()
        arrived(co.at[f], r_c.at[f])

    @pl.when(f == xl)
    def _():
        e_own.start()
        co[f] = ob[xl]

    arrived(co.at[g], r_c.at[g])
    for freq in range(2):
        for comp in range(2):
            coast_ref[:, freq * 2 + comp, :] = co[freq, :, comp * 128 : comp * 128 + 128]

    @pl.when(f == xl)
    def _():
        pltpu.make_async_copy(eb, eb, r_e.at[0]).wait()
        es[...] = jnp.sum(eb[...].reshape(2 * N_PT, 16, 128), axis=0) * (REGIONS / 2048)

        @pl.loop(1, N_PT)
        def _(d):
            remote(es, eo.at[place], r_f.at[0], i, lax.rem(j + d, N_PT)).start()

        pltpu.make_async_copy(es, eo.at[place], r_f.at[0]).start()

    for copy in first + [w_copy] + sent + xh_copies + g_first + [out_far]:
        copy.wait_send()
    for slot in range(6):
        for half in range(2):
            part_copy(slot, half)[1].wait_send()

    def drain(ref):
        remote(ref, ref, r_f.at[0], i, j_core).wait_send()

    drain(en.at[0])
    drain(en.at[1, pl.ds(0, 7)])

    @pl.when(f != xl)
    def _():
        out_near.wait_send()
        drain(es)

    @pl.when(f == xl)
    def _():
        drain(en.at[0])
        drain(en.at[1, pl.ds(0, 7)])

    pltpu.make_async_copy(eo, eo, r_f.at[0]).wait()
    energy_ref[...] = eo[...].reshape(128, REGIONS)


def settle(coast_in, energy_in, coast_ref, energy_ref):
    coast_ref[...] = coast_in[...]
    energy_ref[...] = energy_in[...]


def per_device(slip_counts, spectra, transfer, coast_owner):
    owner = coast_owner.reshape(1, 128)
    vmem = pl.BlockSpec(memory_space=pltpu.VMEM)
    hbm = pl.BlockSpec(memory_space=pl.ANY)
    dma = pltpu.SemaphoreType.DMA
    coast, energy = pl.pallas_call(
        kernel,
        out_shape=(
            jax.ShapeDtypeStruct((128, 4, 128), BF16),
            jax.ShapeDtypeStruct((128, REGIONS), F32),
        ),
        in_specs=[hbm] * 3 + [vmem],
        out_specs=[vmem] * 2,
        scratch_shapes=[
            pltpu.VMEM((128, 2048), jnp.int32),
            pltpu.VMEM((128, 4, 256), BF16),
            pltpu.VMEM((256, 4, 128), BF16),
            pltpu.VMEM((2, 2, 128, 256), BF16),
            pltpu.VMEM((2, 2, 128, 256), BF16),
            pltpu.VMEM((2, 2, 2, 128, 256), BF16),
            pltpu.VMEM((NZ, 2, 2, 128, 256), BF16),
            pltpu.VMEM((NZ, 2, 128, 256), BF16),
            pltpu.VMEM((NZ, 2, 128, 256), BF16),
            pltpu.VMEM((2, NY - 1, 2, 128, 256), BF16),
            pltpu.VMEM((2, 128, 256), BF16),
            pltpu.VMEM((2, 128, 256), BF16),
            pltpu.VMEM((2, 128, 256), F32),
            pltpu.VMEM((NZ, 4, 64, 256), BF16),
            pltpu.VMEM((256, 256), F32),
            pltpu.VMEM((2, 128, 256), BF16),
            pltpu.VMEM((2, 128, 256), BF16),
            pltpu.VMEM((2, 1, 128), jnp.int32),
            pltpu.VMEM((2, NZ, 16, 128), F32),
            pltpu.VMEM((2, N_PT, 16, 128), F32),
            pltpu.VMEM((16, 128), F32),
            pltpu.VMEM((NZ, 16, 128), F32),
            dma((1,)),
            dma((6,)),
            dma((2, 2)),
            dma((NZ, 2, 2)),
            dma((1,)),
            dma((2, NY - 1, 2)),
            dma((2,)),
            dma((NZ, 4)),
            dma((2,)),
            dma((1,)),
            dma((1,)),
            dma((1,)),
        ],
        compiler_params=pltpu.CompilerParams(collective_id=0, has_side_effects=True),
    )(slip_counts, spectra, transfer, owner)
    return pl.pallas_call(
        settle,
        out_shape=(
            jax.ShapeDtypeStruct((128, 4, 128), BF16),
            jax.ShapeDtypeStruct((128, REGIONS), F32),
        ),
        in_specs=[vmem] * 2,
        out_specs=[vmem] * 2,
    )(coast, energy)


def solution(mesh):
    placed = (P("scen", None), P("scen", None, "pt"), P("pt", None, "scen"), P("pt"))
    return jax.shard_map(
        per_device,
        mesh=mesh,
        in_specs=placed,
        out_specs=(P("scen", None, "pt"), P("scen", None)),
        check_vma=False,
    )
```
